32 devices in a mesh: parts: 2 (over y), cell: 4 (over z), grp: 4 (over x, core).
Axes of the slice: x: 2, y: 2, z: 4, core: 2. Of those that a mesh axis runs over, the one named last changes fastest.
Arguments:
- sketch: bfloat16 [98304, 256], P(('parts', 'cell', 'grp')), parts along dimension 0, may hold values from -0.27063294 to 0.27063294, as said below
- slab: bfloat16 [98304, 128], P(('parts', 'cell', 'grp')), parts along dimension 0, may hold values from -6 to 6
Outputs:
- r_factor: float32 [512, 256], P('parts'), parts along dimension 0
- basis: bfloat16 [98304, 256], P(('parts', 'cell', 'grp')), parts along dimension 0
- projected: float32 [512, 128], P(('parts', 'cell'), 'grp'), parts along dimension 0
The draws below stay inside these ranges and needn't reach their ends.
There are 2 independent parts, one for each index of `parts`. The reference program is written for one: setup_inputs(seed, part) draws one part's arguments, and reference() takes and returns one part's arrays. A program takes and returns all parts, laid end to end along the dimension named above; each array names one. Nothing has to cross between parts.
Inputs may be any that keep to these rules, and one draw needn't show every extreme that they name: A scaled random sketch of full column rank.
All inputs are finite; a program needn't handle non-finite values.
Results may differ from the reference program's by a relative error of at most 0.001.
Values sent between devices are 32-bit elements; how exact they have to be, the bound alone decides.
A program may use at most 64 MiB of HBM per device.

```python
import jax
import jax.numpy as jnp
from jax import lax

ROW_DEV = 3072
K = 256
SLAB = 128
ROWS = 49152


def draw_sketch(key, part):
    key_base, key_rows, key_cols = jax.random.split(jax.random.fold_in(key, 17), 3)
    positions = jnp.arange(ROWS, dtype=jnp.float32)
    trend = 1.0 + 2.0 * positions / ROWS
    row_scale = jnp.exp(jax.random.uniform(key_rows, (ROWS,), jnp.float32, 0.0, jnp.log(10.0)))
    col_scale = jnp.exp(jax.random.uniform(key_cols, (K,), jnp.float32, jnp.log(0.5), jnp.log(2.0)))
    base = jnp.clip(jax.random.normal(key_base, (ROWS, K), jnp.float32), -4.0, 4.0)
    values = base * (row_scale * trend)[:, None] * col_scale[None, :] / (4.0 * jnp.sqrt(ROWS * 1.0))
    return values.astype(jnp.bfloat16)


def levels(stream_key, shape, cuts, low, largest):
    level = 1.0
    for position, blocks in cuts:
        steps = jax.random.uniform(jax.random.fold_in(jax.random.fold_in(stream_key, 6), position), (blocks,), jnp.float32, low / len(cuts), largest / len(cuts))
        level = level * jnp.repeat(jnp.exp(steps), shape[position] // blocks).reshape((-1,) + (1,) * (len(shape) - 1 - position))
    return level


def gaussian(key, dims, deviation, limit, shards=(), kind=jnp.bfloat16):
    values = jax.random.normal(key, dims, jnp.float32) * deviation
    if len(shards) > 0:
        values = levels(key, dims, shards, -0.22, 0.18) * values
    return jnp.clip(values, min=-limit, max=limit).astype(kind)


def setup_inputs(seed: int = 0, part: int = 0) -> dict:
    arg_keys = jax.random.split(jax.random.key(seed), 3)
    part_keys = jax.random.split(jax.random.fold_in(arg_keys[2], part), 3)
    sketch = draw_sketch(jax.random.fold_in(jax.random.fold_in(arg_keys[2], part), 71), part)
    slab = gaussian(part_keys[1], (ROWS, SLAB), 1.0, 6.0, ((0, 16),))
    return {"sketch": sketch, "slab": slab}


def gram_of(piece):
    return lax.dot_general(piece.astype(jnp.float32), piece.astype(jnp.float32), (((0,), (0,)), ((), ())), preferred_element_type=jnp.float32)

def reference(sketch, slab):
    sketch_blocks = sketch.reshape(ROWS // ROW_DEV, ROW_DEV, K)
    slab_blocks = slab.reshape(ROWS // ROW_DEV, ROW_DEV, SLAB)

    def add_stats(totals, pieces):
        rows_block, slab_block = pieces
        gram_part = gram_of(rows_block)
        cross_part = lax.dot_general(rows_block.astype(jnp.float32), slab_block.astype(jnp.float32), (((0,), (0,)), ((), ())), preferred_element_type=jnp.float32)
        return ((totals[0] + gram_part, totals[1] + cross_part), None)
    start_totals = (jnp.zeros((K, K), jnp.float32), jnp.zeros((K, SLAB), jnp.float32))
    totals, unused = lax.scan(add_stats, start_totals, (sketch_blocks, slab_blocks))
    gram_sum, cross_sum = totals
    lower_factor = jnp.linalg.cholesky(gram_sum)
    identity = jnp.eye(K, dtype=jnp.float32)
    inverse_lower = lax.linalg.triangular_solve(lower_factor, identity, left_side=True, lower=True)
    inverse_upper = inverse_lower.T

    def solve_block(rows_block):
        exact_rows = jnp.dot(rows_block.astype(jnp.float32), inverse_upper.astype(jnp.float32), precision=lax.Precision.HIGHEST, preferred_element_type=jnp.float32)
        return exact_rows.astype(jnp.bfloat16)
    basis = lax.map(solve_block, sketch_blocks).reshape(ROWS, K)
    projected = lax.linalg.triangular_solve(lower_factor, cross_sum, left_side=True, lower=True)
    return (lower_factor.T, basis, projected)
```

```python
import functools

import jax
import jax.numpy as jnp
from jax import lax
from jax.experimental import pallas as pl
from jax.experimental.pallas import tpu as pltpu
from jax.sharding import PartitionSpec as P

SUB = 8
HIGHEST = lax.Precision.HIGHEST


def dot(a, b, contract, precision=None):
    return lax.dot_general(
        a, b, (contract, ((), ())), precision=precision, preferred_element_type=jnp.float32
    )


def sums_over(a_ref, b_ref, step):
    total = None
    for start in range(0, a_ref.shape[0], step):
        rows = pl.ds(start, min(step, a_ref.shape[0] - start))
        part = dot(a_ref[rows, :], b_ref[rows, :], ((0,), (0,)))
        total = part if total is None else total + part
    return total


def reduce_kernel(
    cells, grps, sketch_ref, slab_ref, gram_ref, cross_ref,
    own_gram, own_cross, grp_gram, grp_cross, cell_gram, cell_cross,
    gs_send, gs_recv, cs_send, cs_recv, gz_send, gz_recv, cz_send, cz_recv, ag_send, ag_recv,
):
    me_c = lax.axis_index("cell")
    me_g = lax.axis_index("grp")
    half = own_gram.shape[1]
    gram_rows = own_gram.shape[0] // grps
    cross_rows = own_cross.shape[0] // grps
    days = cross_rows // 2

    barrier = pltpu.get_barrier_semaphore()
    for d in range(1, grps):
        pl.semaphore_signal(barrier, inc=1, device_id={"grp": lax.rem(me_g + d, grps)}, device_id_type=pl.DeviceIdType.MESH)
    for d in range(1, cells):
        pl.semaphore_signal(barrier, inc=1, device_id={"cell": lax.rem(me_c + d, cells)}, device_id_type=pl.DeviceIdType.MESH)

    gram = sums_over(sketch_ref, sketch_ref, 1024)
    own_gram[0:half, :] = gram[:half, :half]
    own_gram[half : 2 * half, :] = gram[:half, half:]
    own_gram[2 * half :, :] = gram[half:, half:]
    pl.semaphore_wait(barrier, grps + cells - 2)

    def rows_of(ref, index, count):
        return ref.at[pl.ds(pl.multiple_of(index * count, SUB), count), :]

    def to_grps(own, landing, count, send, recv):
        copies = []
        for d in range(1, grps):
            peer = lax.rem(me_g + d, grps)
            copies.append(pltpu.make_async_remote_copy(
                src_ref=rows_of(own, peer, count), dst_ref=landing.at[d - 1],
                send_sem=send.at[d - 1], recv_sem=recv.at[d - 1],
                device_id={"grp": peer}, device_id_type=pl.DeviceIdType.MESH))
        for copy in copies:
            copy.start()
        return copies

    def to_cells(slots, send, recv):
        copies = []
        for d in range(1, cells):
            peer = lax.rem(me_c + d, cells)
            copies.append(pltpu.make_async_remote_copy(
                src_ref=slots.at[me_c], dst_ref=slots.at[me_c],
                send_sem=send.at[d - 1], recv_sem=recv.at[d - 1],
                device_id={"cell": peer}, device_id_type=pl.DeviceIdType.MESH))
        for copy in copies:
            copy.start()
        return copies

    gs = to_grps(own_gram, grp_gram, gram_rows, gs_send, gs_recv)

    cross = sums_over(slab_ref, sketch_ref, 1024)
    for g in range(grps):
        own_cross[g * cross_rows : g * cross_rows + days, :] = cross[g * days : (g + 1) * days, :half]
        own_cross[g * cross_rows + days : (g + 1) * cross_rows, :] = cross[g * days : (g + 1) * days, half:]
    cs = to_grps(own_cross, grp_cross, cross_rows, cs_send, cs_recv)

    def sum_grps(copies, own, landing, count, slots):
        for copy in copies:
            copy.wait_recv()
        total = own[pl.ds(pl.multiple_of(me_g * count, SUB), count), :]
        for d in range(1, grps):
            total = total + landing[d - 1]
        slots[me_c] = total

    sum_grps(gs, own_gram, grp_gram, gram_rows, cell_gram)
    gz = to_cells(cell_gram, gz_send, gz_recv)
    sum_grps(cs, own_cross, grp_cross, cross_rows, cell_cross)
    cz = to_cells(cell_cross, cz_send, cz_recv)

    def sum_cells(copies, slots):
        for copy in copies:
            copy.wait_recv()
        total = slots[0]
        for c in range(1, cells):
            total = total + slots[c]
        return total

    gram_ref[pl.ds(pl.multiple_of(me_g * gram_rows, SUB), gram_rows), :] = sum_cells(gz, cell_gram)
    ag = []
    for d in range(1, grps):
        own = rows_of(gram_ref, me_g, gram_rows)
        ag.append(pltpu.make_async_remote_copy(
            src_ref=own, dst_ref=own, send_sem=ag_send.at[d - 1], recv_sem=ag_recv.at[d - 1],
            device_id={"grp": lax.rem(me_g + d, grps)}, device_id_type=pl.DeviceIdType.MESH))
    for copy in ag:
        copy.start()
    cross_ref[...] = sum_cells(cz, cell_cross)
    for copy in ag:
        copy.wait_recv()
    for copy in gs + cs + gz + cz + ag:
        copy.wait_send()


def reduced(sketch, slab, cells, grps):
    k, days = sketch.shape[1], slab.shape[1]
    half = k // 2
    gram_rows, cross_rows = 3 * half // grps, 2 * days // grps
    if gram_rows % SUB or cross_rows % (2 * SUB) or 3 * half % grps or grps < 2 or cells < 2:
        gram, cross = lax.psum((dot(sketch, sketch, ((0,), (0,))), dot(slab, sketch, ((0,), (0,)))), ("cell", "grp"))
        blocks = jnp.concatenate([gram[:half, :half], gram[:half, half:], gram[half:, half:]], axis=0)
        width = days // grps
        mine = lax.dynamic_slice(cross, (lax.axis_index("grp") * width, 0), (width, k))
        return blocks, jnp.concatenate([mine[:, :half], mine[:, half:]], axis=0)
    f32 = jnp.float32
    dma = pltpu.SemaphoreType.DMA
    return pl.pallas_call(
        functools.partial(reduce_kernel, cells, grps),
        out_shape=(jax.ShapeDtypeStruct((3 * half, half), f32), jax.ShapeDtypeStruct((cross_rows, half), f32)),
        in_specs=[pl.BlockSpec(memory_space=pltpu.VMEM)] * 2,
        out_specs=(pl.BlockSpec(memory_space=pltpu.VMEM),) * 2,
        scratch_shapes=[
            pltpu.VMEM((3 * half, half), f32),
            pltpu.VMEM((2 * days, half), f32),
            pltpu.VMEM((grps - 1, gram_rows, half), f32),
            pltpu.VMEM((grps - 1, cross_rows, half), f32),
            pltpu.VMEM((cells, gram_rows, half), f32),
            pltpu.VMEM((cells, cross_rows, half), f32),
        ] + [dma((grps - 1,))] * 4 + [dma((cells - 1,))] * 4 + [dma((grps - 1,))] * 2,
        compiler_params=pltpu.CompilerParams(collective_id=0, has_side_effects=True),
        name="reduce_sums",
    )(sketch, slab)


def factor(block):
    n = block.shape[0]
    shape = (SUB, n)
    tiles = n // SUB
    sub = lax.broadcasted_iota(jnp.int32, shape, 0)
    lane = lax.broadcasted_iota(jnp.int32, shape, 1)
    m = [block[q * SUB : (q + 1) * SUB, :] for q in range(tiles)]
    w = [jnp.where(lane == sub + q * SUB, 1.0, 0.0).astype(jnp.float32) for q in range(tiles)]
    upper, inverse = [], []

    def row(x, j):
        return jnp.broadcast_to(x[j : j + 1, :], shape)

    def col(x, j):
        return jnp.broadcast_to(x[:, j : j + 1], shape)

    for p in range(tiles):
        t, v = m[p], w[p]
        c = [col(t, p * SUB + i) for i in range(SUB)]
        r_t, r_v = jnp.zeros(shape, jnp.float32), jnp.zeros(shape, jnp.float32)
        for j in range(SUB):
            at = sub == j
            pivot = row(c[j], j)
            inv, root = 1.0 / pivot, lax.rsqrt(pivot)
            f = jnp.where(at, -inv, c[j] * inv)
            t_j, v_j = row(t, j), row(v, j)
            r_t = jnp.where(at, t_j * root, r_t)
            r_v = jnp.where(at, v_j * root, r_v)
            t = jnp.where(at, 0.0, t) - f * t_j
            v = jnp.where(at, 0.0, v) - f * v_j
            for i in range(j + 1, SUB):
                c[i] = jnp.where(at, 0.0, c[i]) - f * row(c[i], j)
        upper.append(jnp.where(lane >= sub + p * SUB, r_t, 0.0))
        inverse.append(r_v)
        if p + 1 < tiles:
            t_rows = [row(t, i) for i in range(SUB)]
            v_rows = [row(v, i) for i in range(SUB)]
            for q in range(p + 1, tiles):
                old = m[q]
                new, new_w = old, w[q]
                for i in range(SUB):
                    c_i = col(old, p * SUB + i)
                    new = new - c_i * t_rows[i]
                    new_w = new_w - c_i * v_rows[i]
                m[q], w[q] = new, new_w
    return jnp.concatenate(upper, axis=0), jnp.concatenate(inverse, axis=0)


def factor_kernel(gram_ref, cross_ref, sketch_ref, r_ref, basis_ref, proj_ref, inv_ref):
    half = gram_ref.shape[1]
    days = cross_ref.shape[0] // 2
    r11, w11 = factor(gram_ref[0:half, :])
    r12 = dot(w11, gram_ref[half : 2 * half, :], ((1,), (0,)), HIGHEST)
    r21 = r12.T
    rest = gram_ref[2 * half :, :] - dot(r21, r12, ((1,), (0,)), HIGHEST)
    mixed = dot(r21, w11, ((1,), (0,)), HIGHEST)
    r22, w22 = factor(rest)
    w21 = -dot(w22, mixed, ((1,), (0,)), HIGHEST)
    zero = jnp.zeros((half, half), jnp.float32)
    r_ref[0:half, 0:half] = r11
    r_ref[0:half, half:] = r12
    r_ref[half:, 0:half] = zero
    r_ref[half:, half:] = r22
    inv_ref[0:half, 0:half] = w11
    inv_ref[0:half, half:] = zero
    inv_ref[half:, 0:half] = w21
    inv_ref[half:, half:] = w22
    rows = proj_ref.shape[0]
    mine = inv_ref[pl.ds(pl.multiple_of(lax.axis_index("cell") * rows, SUB), rows), :]
    proj_ref[...] = dot(mine[:, :half], cross_ref[0:days, :], ((1,), (1,)), HIGHEST) + dot(
        mine[:, half:], cross_ref[days:, :], ((1,), (1,)), HIGHEST)
    whole = inv_ref[...]
    high = whole.astype(jnp.bfloat16)
    low = (whole - high.astype(jnp.float32)).astype(jnp.bfloat16)
    total = sketch_ref.shape[0]
    step = min(512, total)

    for start in range(0, total, step):
        part = sketch_ref[start : start + step, :]
        exact = dot(part, high, ((1,), (1,))) + dot(part, low, ((1,), (1,)))
        basis_ref[start : start + step, :] = exact.astype(jnp.bfloat16)


def local(cells, grps, sketch, slab):
    k, days = sketch.shape[1], slab.shape[1]
    blocks, cross = reduced(sketch, slab, cells, grps)
    vmem = pl.BlockSpec(memory_space=pltpu.VMEM)
    return pl.pallas_call(
        factor_kernel,
        out_shape=(
            jax.ShapeDtypeStruct((k, k), jnp.float32),
            jax.ShapeDtypeStruct(sketch.shape, jnp.bfloat16),
            jax.ShapeDtypeStruct((k // cells, days // grps), jnp.float32),
        ),
        in_specs=[vmem] * 3,
        out_specs=(vmem,) * 3,
        scratch_shapes=[pltpu.VMEM((k, k), jnp.float32)],
        name="factor_and_basis",
    )(blocks, cross, sketch)


def solution(mesh):
    cells, grps = mesh.shape["cell"], mesh.shape["grp"]
    in_specs = (P(("parts", "cell", "grp"), None), P(("parts", "cell", "grp"), None))
    out_specs = (P("parts", None), P(("parts", "cell", "grp"), None), P(("parts", "cell"), "grp"))
    return jax.shard_map(
        functools.partial(local, cells, grps), mesh=mesh, in_specs=in_specs, out_specs=out_specs, check_vma=False)
```

```python
import functools

import jax
import jax.numpy as jnp
from jax import lax
from jax.experimental import pallas as pl
from jax.experimental.pallas import tpu as pltpu
from jax.sharding import PartitionSpec as P

SUB = 8
SUM_STEP = 768
BASIS_STEP = 512
HIGHEST = lax.Precision.HIGHEST


def dot(a, b, contract, precision=None):
    return lax.dot_general(
        a, b, (contract, ((), ())), precision=precision, preferred_element_type=jnp.float32
    )


def chunks_of(total, step):
    return [pl.ds(start, min(step, total - start)) for start in range(0, total, step)]


def sums_over(a_ref, b_ref, loads):
    total = None
    for rows, load in loads:
        load.wait()
        part = dot(a_ref[rows, :], b_ref[rows, :], ((0,), (0,)))
        total = part if total is None else total + part
    return total


def reduce_kernel(
    cells, grps, sketch_hbm, slab_hbm, gram_ref, cross_ref,
    sketch_ref, slab_ref, sketch_sems, slab_sems,
    own_gram, own_cross, grp_gram, grp_cross, cell_gram, cell_cross,
    gs_send, gs_recv, cs_send, cs_recv, gz_send, gz_recv, cz_send, cz_recv, ag_send, ag_recv,
):
    def loading(source, target, sems):
        loads = []
        for i, rows in enumerate(chunks_of(source.shape[0], SUM_STEP)):
            load = pltpu.make_async_copy(source.at[rows, :], target.at[rows, :], sems.at[i])
            load.start()
            loads.append((rows, load))
        return loads

    sketch_loads = loading(sketch_hbm, sketch_ref, sketch_sems)
    slab_loads = loading(slab_hbm, slab_ref, slab_sems)
    me_c = lax.axis_index("cell")
    me_g = lax.axis_index("grp")
    half = own_gram.shape[1]
    gram_rows = own_gram.shape[0] // grps
    cross_rows = own_cross.shape[0] // grps
    days = cross_rows // 2

    barrier = pltpu.get_barrier_semaphore()
    for d in range(1, grps):
        pl.semaphore_signal(barrier, inc=1, device_id={"grp": lax.rem(me_g + d, grps)}, device_id_type=pl.DeviceIdType.MESH)
    for d in range(1, cells):
        pl.semaphore_signal(barrier, inc=1, device_id={"cell": lax.rem(me_c + d, cells)}, device_id_type=pl.DeviceIdType.MESH)

    gram = sums_over(sketch_ref, sketch_ref, sketch_loads)
    own_gram[0:half, :] = gram[:half, :half]
    own_gram[half : 2 * half, :] = gram[:half, half:]
    own_gram[2 * half :, :] = gram[half:, half:]
    pl.semaphore_wait(barrier, grps + cells - 2)

    def rows_of(ref, index, count):
        return ref.at[pl.ds(pl.multiple_of(index * count, SUB), count), :]

    def to_grps(own, landing, count, send, recv):
        copies = []
        for d in range(1, grps):
            peer = lax.rem(me_g + d, grps)
            copies.append(pltpu.make_async_remote_copy(
                src_ref=rows_of(own, peer, count), dst_ref=landing.at[d - 1],
                send_sem=send.at[d - 1], recv_sem=recv.at[d - 1],
                device_id={"grp": peer}, device_id_type=pl.DeviceIdType.MESH))
        for copy in copies:
            copy.start()
        return copies

    def to_cells(slots, send, recv):
        copies = []
        for d in range(1, cells):
            peer = lax.rem(me_c + d, cells)
            copies.append(pltpu.make_async_remote_copy(
                src_ref=slots.at[me_c], dst_ref=slots.at[me_c],
                send_sem=send.at[d - 1], recv_sem=recv.at[d - 1],
                device_id={"cell": peer}, device_id_type=pl.DeviceIdType.MESH))
        for copy in copies:
            copy.start()
        return copies

    gs = to_grps(own_gram, grp_gram, gram_rows, gs_send, gs_recv)

    cross = sums_over(slab_ref, sketch_ref, slab_loads)
    for g in range(grps):
        own_cross[g * cross_rows : g * cross_rows + days, :] = cross[g * days : (g + 1) * days, :half]
        own_cross[g * cross_rows + days : (g + 1) * cross_rows, :] = cross[g * days : (g + 1) * days, half:]
    cs = to_grps(own_cross, grp_cross, cross_rows, cs_send, cs_recv)

    def sum_grps(copies, own, landing, count, slots):
        for copy in copies:
            copy.wait_recv()
        total = own[pl.ds(pl.multiple_of(me_g * count, SUB), count), :]
        for d in range(1, grps):
            total = total + landing[d - 1]
        slots[me_c] = total

    sum_grps(gs, own_gram, grp_gram, gram_rows, cell_gram)
    gz = to_cells(cell_gram, gz_send, gz_recv)
    sum_grps(cs, own_cross, grp_cross, cross_rows, cell_cross)
    cz = to_cells(cell_cross, cz_send, cz_recv)

    def sum_cells(copies, slots):
        for copy in copies:
            copy.wait_recv()
        total = slots[0]
        for c in range(1, cells):
            total = total + slots[c]
        return total

    gram_ref[pl.ds(pl.multiple_of(me_g * gram_rows, SUB), gram_rows), :] = sum_cells(gz, cell_gram)
    ag = []
    for d in range(1, grps):
        own = rows_of(gram_ref, me_g, gram_rows)
        ag.append(pltpu.make_async_remote_copy(
            src_ref=own, dst_ref=own, send_sem=ag_send.at[d - 1], recv_sem=ag_recv.at[d - 1],
            device_id={"grp": lax.rem(me_g + d, grps)}, device_id_type=pl.DeviceIdType.MESH))
    for copy in ag:
        copy.start()
    cross_ref[...] = sum_cells(cz, cell_cross)
    for copy in ag:
        copy.wait_recv()
    for copy in gs + cs + gz + cz + ag:
        copy.wait_send()


def reduced(sketch, slab, cells, grps):
    k, days = sketch.shape[1], slab.shape[1]
    half = k // 2
    gram_rows, cross_rows = 3 * half // grps, 2 * days // grps
    if gram_rows % SUB or cross_rows % (2 * SUB) or 3 * half % grps or grps < 2 or cells < 2:
        gram, cross = lax.psum((dot(sketch, sketch, ((0,), (0,))), dot(slab, sketch, ((0,), (0,)))), ("cell", "grp"))
        blocks = jnp.concatenate([gram[:half, :half], gram[:half, half:], gram[half:, half:]], axis=0)
        width = days // grps
        mine = lax.dynamic_slice(cross, (lax.axis_index("grp") * width, 0), (width, k))
        return blocks, jnp.concatenate([mine[:, :half], mine[:, half:]], axis=0)
    f32 = jnp.float32
    dma = pltpu.SemaphoreType.DMA
    return pl.pallas_call(
        functools.partial(reduce_kernel, cells, grps),
        out_shape=(jax.ShapeDtypeStruct((3 * half, half), f32), jax.ShapeDtypeStruct((cross_rows, half), f32)),
        in_specs=[pl.BlockSpec(memory_space=pl.ANY)] * 2,
        out_specs=(pl.BlockSpec(memory_space=pltpu.VMEM),) * 2,
        scratch_shapes=[
            pltpu.VMEM(sketch.shape, sketch.dtype),
            pltpu.VMEM(slab.shape, slab.dtype),
            dma((len(chunks_of(sketch.shape[0], SUM_STEP)),)),
            dma((len(chunks_of(slab.shape[0], SUM_STEP)),)),
            pltpu.VMEM((3 * half, half), f32),
            pltpu.VMEM((2 * days, half), f32),
            pltpu.VMEM((grps - 1, gram_rows, half), f32),
            pltpu.VMEM((grps - 1, cross_rows, half), f32),
            pltpu.VMEM((cells, gram_rows, half), f32),
            pltpu.VMEM((cells, cross_rows, half), f32),
        ] + [dma((grps - 1,))] * 4 + [dma((cells - 1,))] * 4 + [dma((grps - 1,))] * 2,
        compiler_params=pltpu.CompilerParams(collective_id=0, has_side_effects=True),
        name="reduce_sums",
    )(sketch, slab)


def tree(terms):
    while len(terms) > 1:
        terms = [a + b for a, b in zip(terms[::2], terms[1::2])]
    return terms[0]


def factor(block):
    n = block.shape[0]
    shape = (SUB, n)
    tiles = n // SUB
    sub = lax.broadcasted_iota(jnp.int32, shape, 0)
    lane = lax.broadcasted_iota(jnp.int32, shape, 1)
    m = [block[q * SUB : (q + 1) * SUB, :] for q in range(tiles)]
    w = [jnp.where(lane == sub + q * SUB, 1.0, 0.0).astype(jnp.float32) for q in range(tiles)]
    upper, inverse = [], []

    def row(x, j):
        return jnp.broadcast_to(x[j : j + 1, :], shape)

    def col(x, j):
        return jnp.broadcast_to(x[:, j : j + 1], shape)

    for p in range(tiles):
        t, v = m[p], w[p]
        c = [col(t, p * SUB + i) for i in range(SUB)]
        s = {(j, i): row(c[i], j) for i in range(SUB) for j in range(i + 1)}
        r_t, r_v = jnp.zeros(shape, jnp.float32), jnp.zeros(shape, jnp.float32)
        for j in range(SUB):
            at = sub == j
            pivot = s[j, j]
            inv, root = 1.0 / pivot, lax.rsqrt(pivot)
            f = jnp.where(at, -inv, c[j] * inv)
            t_j, v_j = row(t, j), row(v, j)
            r_t = jnp.where(at, t_j * root, r_t)
            r_v = jnp.where(at, v_j * root, r_v)
            t = jnp.where(at, 0.0, t) - f * t_j
            v = jnp.where(at, 0.0, v) - f * v_j
            scaled = {i: s[j, i] * inv for i in range(j + 1, SUB)}
            for i in range(j + 1, SUB):
                c[i] = jnp.where(at, 0.0, c[i]) - f * s[j, i]
                for h in range(j + 1, i + 1):
                    s[h, i] = s[h, i] - scaled[h] * s[j, i]
        upper.append(jnp.where(lane >= sub + p * SUB, r_t, 0.0))
        inverse.append(r_v)
        if p + 1 < tiles:
            t_rows = [row(t, i) for i in range(SUB)]
            v_rows = [row(v, i) for i in range(SUB)]
            for q in range(p + 1, tiles):
                cols = [col(m[q], p * SUB + i) for i in range(SUB)]
                m[q] = m[q] - tree([a * b for a, b in zip(cols, t_rows)])
                w[q] = w[q] - tree([a * b for a, b in zip(cols, v_rows)])
    return jnp.concatenate(upper, axis=0), jnp.concatenate(inverse, axis=0)


def factor_kernel(
    gram_ref, cross_ref, sketch_hbm, r_ref, basis_hbm, proj_ref,
    inv_ref, sketch_ref, basis_ref, load_sem, store_sems,
):
    load = pltpu.make_async_copy(sketch_hbm, sketch_ref, load_sem)
    load.start()
    half = gram_ref.shape[1]
    days = cross_ref.shape[0] // 2
    r11, w11 = factor(gram_ref[0:half, :])
    r12 = dot(w11, gram_ref[half : 2 * half, :], ((1,), (0,)), HIGHEST)
    r21 = r12.T
    rest = gram_ref[2 * half :, :] - dot(r21, r12, ((1,), (0,)), HIGHEST)
    mixed = dot(r21, w11, ((1,), (0,)), HIGHEST)
    r22, w22 = factor(rest)
    w21 = -dot(w22, mixed, ((1,), (0,)), HIGHEST)
    zero = jnp.zeros((half, half), jnp.float32)
    r_ref[0:half, 0:half] = r11
    r_ref[0:half, half:] = r12
    r_ref[half:, 0:half] = zero
    r_ref[half:, half:] = r22
    inv_ref[0:half, 0:half] = w11
    inv_ref[0:half, half:] = zero
    inv_ref[half:, 0:half] = w21
    inv_ref[half:, half:] = w22
    rows = proj_ref.shape[1]
    mine = inv_ref[pl.ds(pl.multiple_of(lax.axis_index("cell") * rows, SUB), rows), :]
    proj_ref[...] = dot(cross_ref[0:days, :], mine[:, :half], ((1,), (1,)), HIGHEST) + dot(
        cross_ref[days:, :], mine[:, half:], ((1,), (1,)), HIGHEST)
    whole = inv_ref[...]
    high = whole.astype(jnp.bfloat16)
    low = (whole - high.astype(jnp.float32)).astype(jnp.bfloat16)
    load.wait()
    stores = []
    for rows in chunks_of(sketch_ref.shape[0], BASIS_STEP):
        part = sketch_ref[rows, :]
        exact = dot(part, high, ((1,), (1,))) + dot(part, low, ((1,), (1,)))
        basis_ref[rows, :] = exact.astype(jnp.bfloat16)
        stores.append(pltpu.make_async_copy(basis_ref.at[rows, :], basis_hbm.at[rows, :], store_sems.at[len(stores)]))
        stores[-1].start()
    for store in stores:
        store.wait()


def local(cells, grps, sketch, slab):
    k, days = sketch.shape[1], slab.shape[1]
    blocks, cross = reduced(sketch, slab, cells, grps)
    vmem = pl.BlockSpec(memory_space=pltpu.VMEM)
    hbm = pl.BlockSpec(memory_space=pl.ANY)
    r_factor, basis, projected = pl.pallas_call(
        factor_kernel,
        out_shape=(
            jax.ShapeDtypeStruct((k, k), jnp.float32),
            jax.ShapeDtypeStruct(sketch.shape, jnp.bfloat16),
            jax.ShapeDtypeStruct((days // grps, k // cells), jnp.float32),
        ),
        in_specs=[vmem, vmem, hbm],
        out_specs=(vmem, hbm, vmem),
        scratch_shapes=[
            pltpu.VMEM((k, k), jnp.float32),
            pltpu.VMEM(sketch.shape, jnp.bfloat16),
            pltpu.VMEM(sketch.shape, jnp.bfloat16),
            pltpu.SemaphoreType.DMA,
            pltpu.SemaphoreType.DMA((len(chunks_of(sketch.shape[0], BASIS_STEP)),)),
        ],
        name="factor_and_basis",
    )(blocks, cross, sketch)
    return r_factor, basis, projected.T


def solution(mesh):
    cells, grps = mesh.shape["cell"], mesh.shape["grp"]
    in_specs = (P(("parts", "cell", "grp"), None), P(("parts", "cell", "grp"), None))
    out_specs = (P("parts", None), P(("parts", "cell", "grp"), None), P(("parts", "cell"), "grp"))
    return jax.shard_map(
        functools.partial(local, cells, grps), mesh=mesh, in_specs=in_specs, out_specs=out_specs, check_vma=False)
```

```python
import functools

import jax
import jax.numpy as jnp
from jax import lax
from jax.experimental import pallas as pl
from jax.experimental.pallas import tpu as pltpu
from jax.sharding import PartitionSpec as P

SUB = 8
BASE = 64
SUM_STEP = 768
BASIS_STEP = 512
HIGHEST = lax.Precision.HIGHEST


def dot(a, b, contract, precision=None):
    return lax.dot_general(
        a, b, (contract, ((), ())), precision=precision, preferred_element_type=jnp.float32
    )


def chunks_of(total, step):
    return [pl.ds(start, min(step, total - start)) for start in range(0, total, step)]


def sums_over(a_ref, b_ref, loads):
    total = None
    for rows, load in loads:
        load.wait()
        part = dot(a_ref[rows, :], b_ref[rows, :], ((0,), (0,)))
        total = part if total is None else total + part
    return total


def reduce_kernel(
    cells, grps, sketch_hbm, slab_hbm, gram_ref, cross_ref,
    sketch_ref, slab_ref, sketch_sems, slab_sems,
    own_gram, own_cross, grp_gram, grp_cross, cell_gram, cell_cross,
    gs_send, gs_recv, cs_send, cs_recv, gz_send, gz_recv, cz_send, cz_recv, ag_send, ag_recv,
):
    def loading(source, target, sems):
        loads = []
        for i, rows in enumerate(chunks_of(source.shape[0], SUM_STEP)):
            load = pltpu.make_async_copy(source.at[rows, :], target.at[rows, :], sems.at[i])
            load.start()
            loads.append((rows, load))
        return loads

    sketch_loads = loading(sketch_hbm, sketch_ref, sketch_sems)
    slab_loads = loading(slab_hbm, slab_ref, slab_sems)
    me_c = lax.axis_index("cell")
    me_g = lax.axis_index("grp")
    half = own_gram.shape[1]
    gram_rows = own_gram.shape[0] // grps
    cross_rows = own_cross.shape[0] // grps
    days = cross_rows // 2

    barrier = pltpu.get_barrier_semaphore()
    for d in range(1, grps):
        pl.semaphore_signal(barrier, inc=1, device_id={"grp": lax.rem(me_g + d, grps)}, device_id_type=pl.DeviceIdType.MESH)
    for d in range(1, cells):
        pl.semaphore_signal(barrier, inc=1, device_id={"cell": lax.rem(me_c + d, cells)}, device_id_type=pl.DeviceIdType.MESH)

    gram = sums_over(sketch_ref, sketch_ref, sketch_loads)
    own_gram[0:half, :] = gram[:half, :half]
    own_gram[half : 2 * half, :] = gram[:half, half:]
    own_gram[2 * half :, :] = gram[half:, half:]
    pl.semaphore_wait(barrier, grps + cells - 2)

    def rows_of(ref, index, count):
        return ref.at[pl.ds(pl.multiple_of(index * count, SUB), count), :]

    def to_grps(own, landing, count, send, recv):
        copies = []
        for d in range(1, grps):
            peer = lax.rem(me_g + d, grps)
            copies.append(pltpu.make_async_remote_copy(
                src_ref=rows_of(own, peer, count), dst_ref=landing.at[d - 1],
                send_sem=send.at[d - 1], recv_sem=recv.at[d - 1],
                device_id={"grp": peer}, device_id_type=pl.DeviceIdType.MESH))
        for copy in copies:
            copy.start()
        return copies

    def to_cells(slots, send, recv):
        copies = []
        for d in range(1, cells):
            peer = lax.rem(me_c + d, cells)
            copies.append(pltpu.make_async_remote_copy(
                src_ref=slots.at[me_c], dst_ref=slots.at[me_c],
                send_sem=send.at[d - 1], recv_sem=recv.at[d - 1],
                device_id={"cell": peer}, device_id_type=pl.DeviceIdType.MESH))
        for copy in copies:
            copy.start()
        return copies

    gs = to_grps(own_gram, grp_gram, gram_rows, gs_send, gs_recv)

    cross = sums_over(slab_ref, sketch_ref, slab_loads)
    for g in range(grps):
        own_cross[g * cross_rows : g * cross_rows + days, :] = cross[g * days : (g + 1) * days, :half]
        own_cross[g * cross_rows + days : (g + 1) * cross_rows, :] = cross[g * days : (g + 1) * days, half:]
    cs = to_grps(own_cross, grp_cross, cross_rows, cs_send, cs_recv)

    def sum_grps(copies, own, landing, count, slots):
        for copy in copies:
            copy.wait_recv()
        total = own[pl.ds(pl.multiple_of(me_g * count, SUB), count), :]
        for d in range(1, grps):
            total = total + landing[d - 1]
        slots[me_c] = total

    sum_grps(gs, own_gram, grp_gram, gram_rows, cell_gram)
    gz = to_cells(cell_gram, gz_send, gz_recv)
    sum_grps(cs, own_cross, grp_cross, cross_rows, cell_cross)
    cz = to_cells(cell_cross, cz_send, cz_recv)

    def sum_cells(copies, slots):
        for copy in copies:
            copy.wait_recv()
        total = slots[0]
        for c in range(1, cells):
            total = total + slots[c]
        return total

    gram_ref[pl.ds(pl.multiple_of(me_g * gram_rows, SUB), gram_rows), :] = sum_cells(gz, cell_gram)
    ag = []
    for d in range(1, grps):
        own = rows_of(gram_ref, me_g, gram_rows)
        ag.append(pltpu.make_async_remote_copy(
            src_ref=own, dst_ref=own, send_sem=ag_send.at[d - 1], recv_sem=ag_recv.at[d - 1],
            device_id={"grp": lax.rem(me_g + d, grps)}, device_id_type=pl.DeviceIdType.MESH))
    for copy in ag:
        copy.start()
    cross_ref[...] = sum_cells(cz, cell_cross)
    for copy in ag:
        copy.wait_recv()
    for copy in gs + cs + gz + cz + ag:
        copy.wait_send()


def reduced(sketch, slab, cells, grps):
    k, days = sketch.shape[1], slab.shape[1]
    half = k // 2
    gram_rows, cross_rows = 3 * half // grps, 2 * days // grps
    if gram_rows % SUB or cross_rows % (2 * SUB) or 3 * half % grps or grps < 2 or cells < 2:
        gram, cross = lax.psum((dot(sketch, sketch, ((0,), (0,))), dot(slab, sketch, ((0,), (0,)))), ("cell", "grp"))
        blocks = jnp.concatenate([gram[:half, :half], gram[:half, half:], gram[half:, half:]], axis=0)
        width = days // grps
        mine = lax.dynamic_slice(cross, (lax.axis_index("grp") * width, 0), (width, k))
        return blocks, jnp.concatenate([mine[:, :half], mine[:, half:]], axis=0)
    f32 = jnp.float32
    dma = pltpu.SemaphoreType.DMA
    return pl.pallas_call(
        functools.partial(reduce_kernel, cells, grps),
        out_shape=(jax.ShapeDtypeStruct((3 * half, half), f32), jax.ShapeDtypeStruct((cross_rows, half), f32)),
        in_specs=[pl.BlockSpec(memory_space=pl.ANY)] * 2,
        out_specs=(pl.BlockSpec(memory_space=pltpu.VMEM),) * 2,
        scratch_shapes=[
            pltpu.VMEM(sketch.shape, sketch.dtype),
            pltpu.VMEM(slab.shape, slab.dtype),
            dma((len(chunks_of(sketch.shape[0], SUM_STEP)),)),
            dma((len(chunks_of(slab.shape[0], SUM_STEP)),)),
            pltpu.VMEM((3 * half, half), f32),
            pltpu.VMEM((2 * days, half), f32),
            pltpu.VMEM((grps - 1, gram_rows, half), f32),
            pltpu.VMEM((grps - 1, cross_rows, half), f32),
            pltpu.VMEM((cells, gram_rows, half), f32),
            pltpu.VMEM((cells, cross_rows, half), f32),
        ] + [dma((grps - 1,))] * 4 + [dma((cells - 1,))] * 4 + [dma((grps - 1,))] * 2,
        compiler_params=pltpu.CompilerParams(collective_id=0, has_side_effects=True),
        name="reduce_sums",
    )(sketch, slab)


def tree(terms):
    while len(terms) > 1:
        terms = [a + b for a, b in zip(terms[::2], terms[1::2])]
    return terms[0]


def factor_base(block):
    n = block.shape[0]
    shape = (SUB, 2 * n)
    tiles = n // SUB
    sub = lax.broadcasted_iota(jnp.int32, shape, 0)
    lane = lax.broadcasted_iota(jnp.int32, shape, 1)
    eye = jnp.where(
        lax.broadcasted_iota(jnp.int32, (n, n), 0) == lax.broadcasted_iota(jnp.int32, (n, n), 1), 1.0, 0.0)
    wide = jnp.concatenate([block, eye.astype(jnp.float32)], axis=1)
    m = [wide[q * SUB : (q + 1) * SUB, :] for q in range(tiles)]
    done = []

    def row(x, j):
        return jnp.broadcast_to(x[j : j + 1, :], shape)

    def col(x, j):
        return jnp.broadcast_to(x[:, j : j + 1], shape)

    for p in range(tiles):
        t = m[p]
        c = [col(t, p * SUB + i) for i in range(SUB)]
        s = {(j, i): row(c[i], j) for i in range(SUB) for j in range(i + 1)}
        r = jnp.zeros(shape, jnp.float32)
        for j in range(SUB):
            at = sub == j
            pivot = s[j, j]
            inv, root = 1.0 / pivot, lax.rsqrt(pivot)
            f = jnp.where(at, -inv, c[j] * inv)
            t_j = row(t, j)
            r = jnp.where(at, t_j * root, r)
            t = jnp.where(at, 0.0, t) - f * t_j
            scaled = {i: s[j, i] * inv for i in range(j + 1, SUB)}
            for i in range(j + 1, SUB):
                c[i] = jnp.where(at, 0.0, c[i]) - f * s[j, i]
                for h in range(j + 1, i + 1):
                    s[h, i] = s[h, i] - scaled[h] * s[j, i]
        done.append(jnp.where((lane >= sub + p * SUB), r, 0.0))
        if p + 1 < tiles:
            rows = [row(t, i) for i in range(SUB)]
            for q in range(p + 1, tiles):
                m[q] = m[q] - tree([col(m[q], p * SUB + i) * rows[i] for i in range(SUB)])
    done = jnp.concatenate(done, axis=0)
    return done[:, :n], done[:, n:]


def factor(block):
    n = block.shape[0]
    if n <= BASE or n % (2 * SUB):
        return factor_base(block)
    h = n // 2
    r11, w11 = factor(block[:h, :h])
    r12 = dot(w11, block[:h, h:], ((1,), (0,)), HIGHEST)
    r21 = r12.T
    r22, w22 = factor(block[h:, h:] - dot(r21, r12, ((1,), (0,)), HIGHEST))
    w21 = -dot(w22, dot(r21, w11, ((1,), (0,)), HIGHEST), ((1,), (0,)), HIGHEST)
    zero = jnp.zeros((h, h), jnp.float32)
    return (
        jnp.concatenate([jnp.concatenate([r11, r12], axis=1), jnp.concatenate([zero, r22], axis=1)], axis=0),
        jnp.concatenate([jnp.concatenate([w11, zero], axis=1), jnp.concatenate([w21, w22], axis=1)], axis=0),
    )


def factor_kernel(
    gram_ref, cross_ref, sketch_hbm, r_ref, basis_hbm, proj_ref,
    inv_ref, sketch_ref, basis_ref, load_sem, store_sems,
):
    load = pltpu.make_async_copy(sketch_hbm, sketch_ref, load_sem)
    load.start()
    half = gram_ref.shape[1]
    days = cross_ref.shape[0] // 2
    r11, w11 = factor(gram_ref[0:half, :])
    r12 = dot(w11, gram_ref[half : 2 * half, :], ((1,), (0,)), HIGHEST)
    r21 = r12.T
    rest = gram_ref[2 * half :, :] - dot(r21, r12, ((1,), (0,)), HIGHEST)
    mixed = dot(r21, w11, ((1,), (0,)), HIGHEST)
    r22, w22 = factor(rest)
    w21 = -dot(w22, mixed, ((1,), (0,)), HIGHEST)
    zero = jnp.zeros((half, half), jnp.float32)
    r_ref[0:half, 0:half] = r11
    r_ref[0:half, half:] = r12
    r_ref[half:, 0:half] = zero
    r_ref[half:, half:] = r22
    inv_ref[0:half, 0:half] = w11
    inv_ref[0:half, half:] = zero
    inv_ref[half:, 0:half] = w21
    inv_ref[half:, half:] = w22
    rows = proj_ref.shape[1]
    mine = inv_ref[pl.ds(pl.multiple_of(lax.axis_index("cell") * rows, SUB), rows), :]
    proj_ref[...] = dot(cross_ref[0:days, :], mine[:, :half], ((1,), (1,)), HIGHEST) + dot(
        cross_ref[days:, :], mine[:, half:], ((1,), (1,)), HIGHEST)
    whole = inv_ref[...]
    high = whole.astype(jnp.bfloat16)
    low = (whole - high.astype(jnp.float32)).astype(jnp.bfloat16)
    load.wait()
    stores = []
    for rows in chunks_of(sketch_ref.shape[0], BASIS_STEP):
        part = sketch_ref[rows, :]
        exact = dot(part, high, ((1,), (1,))) + dot(part, low, ((1,), (1,)))
        basis_ref[rows, :] = exact.astype(jnp.bfloat16)
        stores.append(pltpu.make_async_copy(basis_ref.at[rows, :], basis_hbm.at[rows, :], store_sems.at[len(stores)]))
        stores[-1].start()
    for store in stores:
        store.wait()


def local(cells, grps, sketch, slab):
    k, days = sketch.shape[1], slab.shape[1]
    blocks, cross = reduced(sketch, slab, cells, grps)
    vmem = pl.BlockSpec(memory_space=pltpu.VMEM)
    hbm = pl.BlockSpec(memory_space=pl.ANY)
    r_factor, basis, projected = pl.pallas_call(
        factor_kernel,
        out_shape=(
            jax.ShapeDtypeStruct((k, k), jnp.float32),
            jax.ShapeDtypeStruct(sketch.shape, jnp.bfloat16),
            jax.ShapeDtypeStruct((days // grps, k // cells), jnp.float32),
        ),
        in_specs=[vmem, vmem, hbm],
        out_specs=(vmem, hbm, vmem),
        scratch_shapes=[
            pltpu.VMEM((k, k), jnp.float32),
            pltpu.VMEM(sketch.shape, jnp.bfloat16),
            pltpu.VMEM(sketch.shape, jnp.bfloat16),
            pltpu.SemaphoreType.DMA,
            pltpu.SemaphoreType.DMA((len(chunks_of(sketch.shape[0], BASIS_STEP)),)),
        ],
        name="factor_and_basis",
    )(blocks, cross, sketch)
    return r_factor, basis, projected.T


def solution(mesh):
    cells, grps = mesh.shape["cell"], mesh.shape["grp"]
    in_specs = (P(("parts", "cell", "grp"), None), P(("parts", "cell", "grp"), None))
    out_specs = (P("parts", None), P(("parts", "cell", "grp"), None), P(("parts", "cell"), "grp"))
    return jax.shard_map(
        functools.partial(local, cells, grps), mesh=mesh, in_specs=in_specs, out_specs=out_specs, check_vma=False)
```

```python
import functools

import jax
import jax.numpy as jnp
from jax import lax
from jax.experimental import pallas as pl
from jax.experimental.pallas import tpu as pltpu
from jax.sharding import PartitionSpec as P

SUB = 8
BASE = 64
SUM_STEP = 768
BASIS_STEP = 512
HIGHEST = lax.Precision.HIGHEST


def dot(a, b, contract, precision=None):
    return lax.dot_general(
        a, b, (contract, ((), ())), precision=precision, preferred_element_type=jnp.float32
    )


def chunks_of(total, step):
    return [pl.ds(start, min(step, total - start)) for start in range(0, total, step)]


def sums_over(a_ref, b_ref, loads):
    total = None
    for rows, load in loads:
        load.wait()
        part = dot(a_ref[rows, :], b_ref[rows, :], ((0,), (0,)))
        total = part if total is None else total + part
    return total


def reduce_kernel(
    cells, grps, sketch_hbm, slab_hbm, gram_ref, cross_ref,
    sketch_ref, slab_ref, sketch_sems, slab_sems,
    own_gram, own_cross, grp_gram, grp_cross, cell_gram, cell_cross,
    gs_send, gs_recv, cs_send, cs_recv, gz_send, gz_recv, cz_send, cz_recv, ag_send, ag_recv,
):
    def loading(source, target, sems):
        loads = []
        for i, rows in enumerate(chunks_of(source.shape[0], SUM_STEP)):
            load = pltpu.make_async_copy(source.at[rows, :], target.at[rows, :], sems.at[i])
            load.start()
            loads.append((rows, load))
        return loads

    sketch_loads = loading(sketch_hbm, sketch_ref, sketch_sems)
    slab_loads = loading(slab_hbm, slab_ref, slab_sems)
    me_c = lax.axis_index("cell")
    me_g = lax.axis_index("grp")
    half = own_gram.shape[1]
    gram_rows = own_gram.shape[0] // grps
    cross_rows = own_cross.shape[0] // grps
    days = cross_rows // 2

    barrier = pltpu.get_barrier_semaphore()
    for d in range(1, grps):
        pl.semaphore_signal(barrier, inc=1, device_id={"grp": lax.rem(me_g + d, grps)}, device_id_type=pl.DeviceIdType.MESH)
    for d in range(1, cells):
        pl.semaphore_signal(barrier, inc=1, device_id={"cell": lax.rem(me_c + d, cells)}, device_id_type=pl.DeviceIdType.MESH)

    gram = sums_over(sketch_ref, sketch_ref, sketch_loads)
    own_gram[0:half, :] = gram[:half, :half]
    own_gram[half : 2 * half, :] = gram[:half, half:]
    own_gram[2 * half :, :] = gram[half:, half:]
    pl.semaphore_wait(barrier, grps + cells - 2)

    def rows_of(ref, index, count):
        return ref.at[pl.ds(pl.multiple_of(index * count, SUB), count), :]

    def to_grps(own, landing, count, send, recv):
        copies = []
        for d in range(1, grps):
            peer = lax.rem(me_g + d, grps)
            copies.append(pltpu.make_async_remote_copy(
                src_ref=rows_of(own, peer, count), dst_ref=landing.at[d - 1],
                send_sem=send.at[d - 1], recv_sem=recv.at[d - 1],
                device_id={"grp": peer}, device_id_type=pl.DeviceIdType.MESH))
        for copy in copies:
            copy.start()
        return copies

    def to_cells(slots, send, recv):
        copies = []
        for d in range(1, cells):
            peer = lax.rem(me_c + d, cells)
            copies.append(pltpu.make_async_remote_copy(
                src_ref=slots.at[me_c], dst_ref=slots.at[me_c],
                send_sem=send.at[d - 1], recv_sem=recv.at[d - 1],
                device_id={"cell": peer}, device_id_type=pl.DeviceIdType.MESH))
        for copy in copies:
            copy.start()
        return copies

    gs = to_grps(own_gram, grp_gram, gram_rows, gs_send, gs_recv)

    cross = sums_over(slab_ref, sketch_ref, slab_loads)
    for g in range(grps):
        own_cross[g * cross_rows : g * cross_rows + days, :] = cross[g * days : (g + 1) * days, :half]
        own_cross[g * cross_rows + days : (g + 1) * cross_rows, :] = cross[g * days : (g + 1) * days, half:]
    cs = to_grps(own_cross, grp_cross, cross_rows, cs_send, cs_recv)

    def sum_grps(copies, own, landing, count, slots):
        for copy in copies:
            copy.wait_recv()
        total = own[pl.ds(pl.multiple_of(me_g * count, SUB), count), :]
        for d in range(1, grps):
            total = total + landing[d - 1]
        slots[me_c] = total

    sum_grps(gs, own_gram, grp_gram, gram_rows, cell_gram)
    gz = to_cells(cell_gram, gz_send, gz_recv)
    sum_grps(cs, own_cross, grp_cross, cross_rows, cell_cross)
    cz = to_cells(cell_cross, cz_send, cz_recv)

    def sum_cells(copies, slots):
        for copy in copies:
            copy.wait_recv()
        total = slots[0]
        for c in range(1, cells):
            total = total + slots[c]
        return total

    gram_ref[pl.ds(pl.multiple_of(me_g * gram_rows, SUB), gram_rows), :] = sum_cells(gz, cell_gram)
    ag = []
    for d in range(1, grps):
        own = rows_of(gram_ref, me_g, gram_rows)
        ag.append(pltpu.make_async_remote_copy(
            src_ref=own, dst_ref=own, send_sem=ag_send.at[d - 1], recv_sem=ag_recv.at[d - 1],
            device_id={"grp": lax.rem(me_g + d, grps)}, device_id_type=pl.DeviceIdType.MESH))
    for copy in ag:
        copy.start()
    cross_ref[...] = sum_cells(cz, cell_cross)
    for copy in ag:
        copy.wait_recv()
    for copy in gs + cs + gz + cz + ag:
        copy.wait_send()


def reduced(sketch, slab, cells, grps):
    k, days = sketch.shape[1], slab.shape[1]
    half = k // 2
    gram_rows, cross_rows = 3 * half // grps, 2 * days // grps
    if gram_rows % SUB or cross_rows % (2 * SUB) or 3 * half % grps or grps < 2 or cells < 2:
        gram, cross = lax.psum((dot(sketch, sketch, ((0,), (0,))), dot(slab, sketch, ((0,), (0,)))), ("cell", "grp"))
        blocks = jnp.concatenate([gram[:half, :half], gram[:half, half:], gram[half:, half:]], axis=0)
        width = days // grps
        mine = lax.dynamic_slice(cross, (lax.axis_index("grp") * width, 0), (width, k))
        return blocks, jnp.concatenate([mine[:, :half], mine[:, half:]], axis=0)
    f32 = jnp.float32
    dma = pltpu.SemaphoreType.DMA
    return pl.pallas_call(
        functools.partial(reduce_kernel, cells, grps),
        out_shape=(jax.ShapeDtypeStruct((3 * half, half), f32), jax.ShapeDtypeStruct((cross_rows, half), f32)),
        in_specs=[pl.BlockSpec(memory_space=pl.ANY)] * 2,
        out_specs=(pl.BlockSpec(memory_space=pltpu.VMEM),) * 2,
        scratch_shapes=[
            pltpu.VMEM(sketch.shape, sketch.dtype),
            pltpu.VMEM(slab.shape, slab.dtype),
            dma((len(chunks_of(sketch.shape[0], SUM_STEP)),)),
            dma((len(chunks_of(slab.shape[0], SUM_STEP)),)),
            pltpu.VMEM((3 * half, half), f32),
            pltpu.VMEM((2 * days, half), f32),
            pltpu.VMEM((grps - 1, gram_rows, half), f32),
            pltpu.VMEM((grps - 1, cross_rows, half), f32),
            pltpu.VMEM((cells, gram_rows, half), f32),
            pltpu.VMEM((cells, cross_rows, half), f32),
        ] + [dma((grps - 1,))] * 4 + [dma((cells - 1,))] * 4 + [dma((grps - 1,))] * 2,
        compiler_params=pltpu.CompilerParams(collective_id=0, has_side_effects=True),
        name="reduce_sums",
    )(sketch, slab)


def tree(terms):
    while len(terms) > 1:
        terms = [a + b for a, b in zip(terms[::2], terms[1::2])]
    return terms[0]


def factor_base(block, ones_ref):
    n = block.shape[0]
    shape = (SUB, 2 * n)
    ones = ones_ref[:, : 2 * n]
    tiles = n // SUB
    sub = lax.broadcasted_iota(jnp.int32, shape, 0)
    lane = lax.broadcasted_iota(jnp.int32, shape, 1)
    eye = jnp.where(
        lax.broadcasted_iota(jnp.int32, (n, n), 0) == lax.broadcasted_iota(jnp.int32, (n, n), 1), 1.0, 0.0)
    wide = jnp.concatenate([block, eye.astype(jnp.float32)], axis=1)
    m = [wide[q * SUB : (q + 1) * SUB, :] for q in range(tiles)]
    done = []

    def row(x, j):
        return jnp.broadcast_to(x[j : j + 1, :], shape)

    def col(x, j):
        return jnp.broadcast_to(x[:, j : j + 1], shape)

    for p in range(tiles):
        t = m[p]
        c = [col(t, p * SUB + i) * ones for i in range(SUB)]
        s = {(j, i): row(c[i], j) for i in range(SUB) for j in range(i + 1)}
        r = jnp.zeros(shape, jnp.float32)
        for j in range(SUB):
            at = sub == j
            pivot = s[j, j]
            inv, root = 1.0 / pivot, lax.rsqrt(pivot)
            f = jnp.where(at, -inv, c[j] * inv)
            t_j = row(t, j)
            r = jnp.where(at, t_j * root, r)
            t = jnp.where(at, 0.0, t) - f * t_j
            scaled = {i: s[j, i] * inv for i in range(j + 1, SUB)}
            for i in range(j + 1, SUB):
                c[i] = jnp.where(at, 0.0, c[i]) - f * s[j, i]
                for h in range(j + 1, i + 1):
                    s[h, i] = s[h, i] - scaled[h] * s[j, i]
        done.append(jnp.where((lane >= sub + p * SUB), r, 0.0))
        if p + 1 < tiles:
            rows = [row(t, i) for i in range(SUB)]
            for q in range(p + 1, tiles):
                m[q] = m[q] - tree([col(m[q], p * SUB + i) * rows[i] for i in range(SUB)])
    done = jnp.concatenate(done, axis=0)
    return done[:, :n], done[:, n:]


def factor(block, ones_ref):
    n = block.shape[0]
    if n <= BASE or n % (2 * SUB):
        return factor_base(block, ones_ref)
    h = n // 2
    r11, w11 = factor(block[:h, :h], ones_ref)
    r12 = dot(w11, block[:h, h:], ((1,), (0,)), HIGHEST)
    r21 = r12.T
    r22, w22 = factor(block[h:, h:] - dot(r21, r12, ((1,), (0,)), HIGHEST), ones_ref)
    w21 = -dot(w22, dot(r21, w11, ((1,), (0,)), HIGHEST), ((1,), (0,)), HIGHEST)
    zero = jnp.zeros((h, h), jnp.float32)
    return (
        jnp.concatenate([jnp.concatenate([r11, r12], axis=1), jnp.concatenate([zero, r22], axis=1)], axis=0),
        jnp.concatenate([jnp.concatenate([w11, zero], axis=1), jnp.concatenate([w21, w22], axis=1)], axis=0),
    )


def factor_kernel(
    gram_ref, cross_ref, sketch_hbm, r_ref, basis_hbm, proj_ref,
    inv_ref, ones_ref, sketch_ref, basis_ref, load_sem, store_sems,
):
    load = pltpu.make_async_copy(sketch_hbm, sketch_ref, load_sem)
    load.start()
    ones_ref[...] = jnp.ones_like(ones_ref)
    half = gram_ref.shape[1]
    days = cross_ref.shape[0] // 2
    r11, w11 = factor(gram_ref[0:half, :], ones_ref)
    r12 = dot(w11, gram_ref[half : 2 * half, :], ((1,), (0,)), HIGHEST)
    r21 = r12.T
    rest = gram_ref[2 * half :, :] - dot(r21, r12, ((1,), (0,)), HIGHEST)
    mixed = dot(r21, w11, ((1,), (0,)), HIGHEST)
    r22, w22 = factor(rest, ones_ref)
    w21 = -dot(w22, mixed, ((1,), (0,)), HIGHEST)
    zero = jnp.zeros((half, half), jnp.float32)
    r_ref[0:half, 0:half] = r11
    r_ref[0:half, half:] = r12
    r_ref[half:, 0:half] = zero
    r_ref[half:, half:] = r22
    inv_ref[0:half, 0:half] = w11
    inv_ref[0:half, half:] = zero
    inv_ref[half:, 0:half] = w21
    inv_ref[half:, half:] = w22
    rows = proj_ref.shape[1]
    mine = inv_ref[pl.ds(pl.multiple_of(lax.axis_index("cell") * rows, SUB), rows), :]
    proj_ref[...] = dot(cross_ref[0:days, :], mine[:, :half], ((1,), (1,)), HIGHEST) + dot(
        cross_ref[days:, :], mine[:, half:], ((1,), (1,)), HIGHEST)
    whole = inv_ref[...]
    high = whole.astype(jnp.bfloat16)
    low = (whole - high.astype(jnp.float32)).astype(jnp.bfloat16)
    load.wait()
    stores = []
    for rows in chunks_of(sketch_ref.shape[0], BASIS_STEP):
        part = sketch_ref[rows, :]
        exact = dot(part, high, ((1,), (1,))) + dot(part, low, ((1,), (1,)))
        basis_ref[rows, :] = exact.astype(jnp.bfloat16)
        stores.append(pltpu.make_async_copy(basis_ref.at[rows, :], basis_hbm.at[rows, :], store_sems.at[len(stores)]))
        stores[-1].start()
    for store in stores:
        store.wait()


def local(cells, grps, sketch, slab):
    k, days = sketch.shape[1], slab.shape[1]
    blocks, cross = reduced(sketch, slab, cells, grps)
    vmem = pl.BlockSpec(memory_space=pltpu.VMEM)
    hbm = pl.BlockSpec(memory_space=pl.ANY)
    r_factor, basis, projected = pl.pallas_call(
        factor_kernel,
        out_shape=(
            jax.ShapeDtypeStruct((k, k), jnp.float32),
            jax.ShapeDtypeStruct(sketch.shape, jnp.bfloat16),
            jax.ShapeDtypeStruct((days // grps, k // cells), jnp.float32),
        ),
        in_specs=[vmem, vmem, hbm],
        out_specs=(vmem, hbm, vmem),
        scratch_shapes=[
            pltpu.VMEM((k, k), jnp.float32),
            pltpu.VMEM((SUB, k), jnp.float32),
            pltpu.VMEM(sketch.shape, jnp.bfloat16),
            pltpu.VMEM(sketch.shape, jnp.bfloat16),
            pltpu.SemaphoreType.DMA,
            pltpu.SemaphoreType.DMA((len(chunks_of(sketch.shape[0], BASIS_STEP)),)),
        ],
        name="factor_and_basis",
    )(blocks, cross, sketch)
    return r_factor, basis, projected.T


def solution(mesh):
    cells, grps = mesh.shape["cell"], mesh.shape["grp"]
    in_specs = (P(("parts", "cell", "grp"), None), P(("parts", "cell", "grp"), None))
    out_specs = (P("parts", None), P(("parts", "cell", "grp"), None), P(("parts", "cell"), "grp"))
    return jax.shard_map(
        functools.partial(local, cells, grps), mesh=mesh, in_specs=in_specs, out_specs=out_specs, check_vma=False)
```

```python
import functools

import jax
import jax.numpy as jnp
from jax import lax
from jax.experimental import pallas as pl
from jax.experimental.pallas import tpu as pltpu
from jax.sharding import PartitionSpec as P

SUB = 8
BASE = 64
SUM_STEP = 768
BASIS_STEP = 512
HIGHEST = lax.Precision.HIGHEST


def dot(a, b, contract, precision=None):
    return lax.dot_general(
        a, b, (contract, ((), ())), precision=precision, preferred_element_type=jnp.float32
    )


def chunks_of(total, step):
    return [pl.ds(start, min(step, total - start)) for start in range(0, total, step)]


def sums_over(a_ref, b_ref, loads):
    total = None
    for rows, load in loads:
        load.wait()
        part = dot(a_ref[rows, :], b_ref[rows, :], ((0,), (0,)))
        total = part if total is None else total + part
    return total


def reduce_kernel(
    cells, grps, sketch_hbm, slab_hbm, gram_ref, cross_ref,
    sketch_ref, slab_ref, sketch_sems, slab_sems,
    own_gram, own_cross, grp_gram, grp_cross, cell_gram, cell_cross,
    gs_send, gs_recv, cs_send, cs_recv, gz_send, gz_recv, cz_send, cz_recv, ag_send, ag_recv,
):
    def loading(source, target, sems):
        loads = []
        for i, rows in enumerate(chunks_of(source.shape[0], SUM_STEP)):
            load = pltpu.make_async_copy(source.at[rows, :], target.at[rows, :], sems.at[i])
            load.start()
            loads.append((rows, load))
        return loads

    sketch_loads = loading(sketch_hbm, sketch_ref, sketch_sems)
    slab_loads = loading(slab_hbm, slab_ref, slab_sems)
    me_c = lax.axis_index("cell")
    me_g = lax.axis_index("grp")
    half = own_gram.shape[1]
    gram_rows = own_gram.shape[0] // grps
    cross_rows = own_cross.shape[0] // grps
    days = cross_rows // 2

    barrier = pltpu.get_barrier_semaphore()
    for d in range(1, grps):
        pl.semaphore_signal(barrier, inc=1, device_id={"grp": lax.rem(me_g + d, grps)}, device_id_type=pl.DeviceIdType.MESH)
    for d in range(1, cells):
        pl.semaphore_signal(barrier, inc=1, device_id={"cell": lax.rem(me_c + d, cells)}, device_id_type=pl.DeviceIdType.MESH)

    gram = sums_over(sketch_ref, sketch_ref, sketch_loads)
    own_gram[0:half, :] = gram[:half, :half]
    own_gram[half : 2 * half, :] = gram[:half, half:]
    own_gram[2 * half :, :] = gram[half:, half:]
    pl.semaphore_wait(barrier, grps + cells - 2)

    def rows_of(ref, index, count):
        return ref.at[pl.ds(pl.multiple_of(index * count, SUB), count), :]

    def to_grps(own, landing, count, send, recv):
        copies = []
        for d in range(1, grps):
            peer = lax.rem(me_g + d, grps)
            copies.append(pltpu.make_async_remote_copy(
                src_ref=rows_of(own, peer, count), dst_ref=landing.at[d - 1],
                send_sem=send.at[d - 1], recv_sem=recv.at[d - 1],
                device_id={"grp": peer}, device_id_type=pl.DeviceIdType.MESH))
        for copy in copies:
            copy.start()
        return copies

    def to_cells(slots, send, recv):
        copies = []
        for d in range(1, cells):
            peer = lax.rem(me_c + d, cells)
            copies.append(pltpu.make_async_remote_copy(
                src_ref=slots.at[me_c], dst_ref=slots.at[me_c],
                send_sem=send.at[d - 1], recv_sem=recv.at[d - 1],
                device_id={"cell": peer}, device_id_type=pl.DeviceIdType.MESH))
        for copy in copies:
            copy.start()
        return copies

    gs = to_grps(own_gram, grp_gram, gram_rows, gs_send, gs_recv)

    cross = sums_over(slab_ref, sketch_ref, slab_loads)
    for g in range(grps):
        own_cross[g * cross_rows : g * cross_rows + days, :] = cross[g * days : (g + 1) * days, :half]
        own_cross[g * cross_rows + days : (g + 1) * cross_rows, :] = cross[g * days : (g + 1) * days, half:]
    cs = to_grps(own_cross, grp_cross, cross_rows, cs_send, cs_recv)

    def sum_grps(copies, own, landing, count, slots):
        for copy in copies:
            copy.wait_recv()
        total = own[pl.ds(pl.multiple_of(me_g * count, SUB), count), :]
        for d in range(1, grps):
            total = total + landing[d - 1]
        slots[me_c] = total

    sum_grps(gs, own_gram, grp_gram, gram_rows, cell_gram)
    gz = to_cells(cell_gram, gz_send, gz_recv)
    sum_grps(cs, own_cross, grp_cross, cross_rows, cell_cross)
    cz = to_cells(cell_cross, cz_send, cz_recv)

    def sum_cells(copies, slots):
        for copy in copies:
            copy.wait_recv()
        total = slots[0]
        for c in range(1, cells):
            total = total + slots[c]
        return total

    gram_ref[pl.ds(pl.multiple_of(me_g * gram_rows, SUB), gram_rows), :] = sum_cells(gz, cell_gram)
    ag = []
    for d in range(1, grps):
        own = rows_of(gram_ref, me_g, gram_rows)
        ag.append(pltpu.make_async_remote_copy(
            src_ref=own, dst_ref=own, send_sem=ag_send.at[d - 1], recv_sem=ag_recv.at[d - 1],
            device_id={"grp": lax.rem(me_g + d, grps)}, device_id_type=pl.DeviceIdType.MESH))
    for copy in ag:
        copy.start()
    cross_ref[...] = sum_cells(cz, cell_cross)
    for copy in ag:
        copy.wait_recv()
    for copy in gs + cs + gz + cz + ag:
        copy.wait_send()


def reduced(sketch, slab, cells, grps):
    k, days = sketch.shape[1], slab.shape[1]
    half = k // 2
    gram_rows, cross_rows = 3 * half // grps, 2 * days // grps
    if gram_rows % SUB or cross_rows % (2 * SUB) or 3 * half % grps or grps < 2 or cells < 2:
        gram, cross = lax.psum((dot(sketch, sketch, ((0,), (0,))), dot(slab, sketch, ((0,), (0,)))), ("cell", "grp"))
        blocks = jnp.concatenate([gram[:half, :half], gram[:half, half:], gram[half:, half:]], axis=0)
        width = days // grps
        mine = lax.dynamic_slice(cross, (lax.axis_index("grp") * width, 0), (width, k))
        return blocks, jnp.concatenate([mine[:, :half], mine[:, half:]], axis=0)
    f32 = jnp.float32
    dma = pltpu.SemaphoreType.DMA
    return pl.pallas_call(
        functools.partial(reduce_kernel, cells, grps),
        out_shape=(jax.ShapeDtypeStruct((3 * half, half), f32), jax.ShapeDtypeStruct((cross_rows, half), f32)),
        in_specs=[pl.BlockSpec(memory_space=pl.ANY)] * 2,
        out_specs=(pl.BlockSpec(memory_space=pltpu.VMEM),) * 2,
        scratch_shapes=[
            pltpu.VMEM(sketch.shape, sketch.dtype),
            pltpu.VMEM(slab.shape, slab.dtype),
            dma((len(chunks_of(sketch.shape[0], SUM_STEP)),)),
            dma((len(chunks_of(slab.shape[0], SUM_STEP)),)),
            pltpu.VMEM((3 * half, half), f32),
            pltpu.VMEM((2 * days, half), f32),
            pltpu.VMEM((grps - 1, gram_rows, half), f32),
            pltpu.VMEM((grps - 1, cross_rows, half), f32),
            pltpu.VMEM((cells, gram_rows, half), f32),
            pltpu.VMEM((cells, cross_rows, half), f32),
        ] + [dma((grps - 1,))] * 4 + [dma((cells - 1,))] * 4 + [dma((grps - 1,))] * 2,
        compiler_params=pltpu.CompilerParams(collective_id=0, has_side_effects=True),
        name="reduce_sums",
    )(sketch, slab)


def tree(terms):
    while len(terms) > 1:
        terms = [a + b for a, b in zip(terms[::2], terms[1::2])]
    return terms[0]


def factor_base(block, ones_ref):
    n = block.shape[0]
    shape = (SUB, 2 * n)
    ones = ones_ref[:, : 2 * n]
    tiles = n // SUB
    sub = lax.broadcasted_iota(jnp.int32, shape, 0)
    lane = lax.broadcasted_iota(jnp.int32, shape, 1)
    eye = jnp.where(
        lax.broadcasted_iota(jnp.int32, (n, n), 0) == lax.broadcasted_iota(jnp.int32, (n, n), 1), 1.0, 0.0)
    wide = jnp.concatenate([block, eye.astype(jnp.float32)], axis=1)
    m = [wide[q * SUB : (q + 1) * SUB, :] for q in range(tiles)]
    done = []

    def row(x, j):
        return jnp.broadcast_to(x[j : j + 1, :], shape)

    def col(x, j):
        return jnp.broadcast_to(x[:, j : j + 1], shape)

    for p in range(tiles):
        t = m[p]
        c = [col(t, p * SUB + i) * ones for i in range(SUB)]
        s = {(j, i): row(c[i], j) for i in range(SUB) for j in range(i + 1)}
        r = jnp.zeros(shape, jnp.float32)
        for j in range(SUB):
            at = sub == j
            pivot = s[j, j]
            inv, root = 1.0 / pivot, lax.rsqrt(pivot)
            f = jnp.where(at, -inv, c[j] * inv)
            t_j = row(t, j)
            r = jnp.where(at, t_j * root, r)
            t = jnp.where(at, 0.0, t) - f * t_j
            scaled = {i: s[j, i] * inv for i in range(j + 1, SUB)}
            for i in range(j + 1, SUB):
                c[i] = jnp.where(at, 0.0, c[i]) - f * s[j, i]
                for h in range(j + 1, i + 1):
                    s[h, i] = s[h, i] - scaled[h] * s[j, i]
        done.append(jnp.where((lane >= sub + p * SUB), r, 0.0))
        if p + 1 < tiles:
            rows = [row(t, i) for i in range(SUB)]
            later = range(p + 1, tiles)
            terms = [[col(m[q], p * SUB + i) * rows[i] for q in later] for i in range(SUB)]
            for at, q in enumerate(later):
                m[q] = m[q] - tree([terms[i][at] for i in range(SUB)])
    done = jnp.concatenate(done, axis=0)
    return done[:, :n], done[:, n:]


def factor(block, ones_ref):
    n = block.shape[0]
    if n <= BASE or n % (2 * SUB):
        return factor_base(block, ones_ref)
    h = n // 2
    r11, w11 = factor(block[:h, :h], ones_ref)
    r12 = dot(w11, block[:h, h:], ((1,), (0,)), HIGHEST)
    r21 = r12.T
    r22, w22 = factor(block[h:, h:] - dot(r21, r12, ((1,), (0,)), HIGHEST), ones_ref)
    w21 = -dot(w22, dot(r21, w11, ((1,), (0,)), HIGHEST), ((1,), (0,)), HIGHEST)
    zero = jnp.zeros((h, h), jnp.float32)
    return (
        jnp.concatenate([jnp.concatenate([r11, r12], axis=1), jnp.concatenate([zero, r22], axis=1)], axis=0),
        jnp.concatenate([jnp.concatenate([w11, zero], axis=1), jnp.concatenate([w21, w22], axis=1)], axis=0),
    )


def factor_kernel(
    gram_ref, cross_ref, sketch_hbm, r_ref, basis_hbm, proj_ref,
    inv_ref, ones_ref, sketch_ref, basis_ref, load_sem, store_sems,
):
    load = pltpu.make_async_copy(sketch_hbm, sketch_ref, load_sem)
    load.start()
    ones_ref[...] = jnp.ones_like(ones_ref)
    half = gram_ref.shape[1]
    days = cross_ref.shape[0] // 2
    r11, w11 = factor(gram_ref[0:half, :], ones_ref)
    r12 = dot(w11, gram_ref[half : 2 * half, :], ((1,), (0,)), HIGHEST)
    r21 = r12.T
    rest = gram_ref[2 * half :, :] - dot(r21, r12, ((1,), (0,)), HIGHEST)
    mixed = dot(r21, w11, ((1,), (0,)), HIGHEST)
    r22, w22 = factor(rest, ones_ref)
    w21 = -dot(w22, mixed, ((1,), (0,)), HIGHEST)
    zero = jnp.zeros((half, half), jnp.float32)
    r_ref[0:half, 0:half] = r11
    r_ref[0:half, half:] = r12
    r_ref[half:, 0:half] = zero
    r_ref[half:, half:] = r22
    inv_ref[0:half, 0:half] = w11
    inv_ref[0:half, half:] = zero
    inv_ref[half:, 0:half] = w21
    inv_ref[half:, half:] = w22
    rows = proj_ref.shape[1]
    mine = inv_ref[pl.ds(pl.multiple_of(lax.axis_index("cell") * rows, SUB), rows), :]
    proj_ref[...] = dot(cross_ref[0:days, :], mine[:, :half], ((1,), (1,)), HIGHEST) + dot(
        cross_ref[days:, :], mine[:, half:], ((1,), (1,)), HIGHEST)
    whole = inv_ref[...]
    high = whole.astype(jnp.bfloat16)
    low = (whole - high.astype(jnp.float32)).astype(jnp.bfloat16)
    load.wait()
    stores = []
    for rows in chunks_of(sketch_ref.shape[0], BASIS_STEP):
        part = sketch_ref[rows, :]
        exact = dot(part, high, ((1,), (1,))) + dot(part, low, ((1,), (1,)))
        basis_ref[rows, :] = exact.astype(jnp.bfloat16)
        stores.append(pltpu.make_async_copy(basis_ref.at[rows, :], basis_hbm.at[rows, :], store_sems.at[len(stores)]))
        stores[-1].start()
    for store in stores:
        store.wait()


def local(cells, grps, sketch, slab):
    k, days = sketch.shape[1], slab.shape[1]
    blocks, cross = reduced(sketch, slab, cells, grps)
    vmem = pl.BlockSpec(memory_space=pltpu.VMEM)
    hbm = pl.BlockSpec(memory_space=pl.ANY)
    r_factor, basis, projected = pl.pallas_call(
        factor_kernel,
        out_shape=(
            jax.ShapeDtypeStruct((k, k), jnp.float32),
            jax.ShapeDtypeStruct(sketch.shape, jnp.bfloat16),
            jax.ShapeDtypeStruct((days // grps, k // cells), jnp.float32),
        ),
        in_specs=[vmem, vmem, hbm],
        out_specs=(vmem, hbm, vmem),
        scratch_shapes=[
            pltpu.VMEM((k, k), jnp.float32),
            pltpu.VMEM((SUB, k), jnp.float32),
            pltpu.VMEM(sketch.shape, jnp.bfloat16),
            pltpu.VMEM(sketch.shape, jnp.bfloat16),
            pltpu.SemaphoreType.DMA,
            pltpu.SemaphoreType.DMA((len(chunks_of(sketch.shape[0], BASIS_STEP)),)),
        ],
        name="factor_and_basis",
    )(blocks, cross, sketch)
    return r_factor, basis, projected.T


def solution(mesh):
    cells, grps = mesh.shape["cell"], mesh.shape["grp"]
    in_specs = (P(("parts", "cell", "grp"), None), P(("parts", "cell", "grp"), None))
    out_specs = (P("parts", None), P(("parts", "cell", "grp"), None), P(("parts", "cell"), "grp"))
    return jax.shard_map(
        functools.partial(local, cells, grps), mesh=mesh, in_specs=in_specs, out_specs=out_specs, check_vma=False)
```
